128 devices in a mesh: gx: 8 (over y, core), gy: 16 (over z, x).
Axes of the slice: x: 4, y: 4, z: 4, core: 2. Of those that a mesh axis runs over, the one named last changes fastest.
Arguments:
- charges: bfloat16 [2048, 256, 64], P(('gx', 'gy')), may hold values from -6 to 6
- leaf_basis: bfloat16 [2048, 256, 64], P(('gx', 'gy')), may hold values from -0.375 to 0.375
- transfer: bfloat16 [128, 24, 64, 64], P(('gx', 'gy')), may hold values from -0.5 to 0.5
- near_blocks: bfloat16 [2048, 6, 256, 256], P(('gx', 'gy')), may hold values from -0.15625 to 0.15625
- near_source: int32 [2048, 6], P(('gx', 'gy')), may hold values from 0 to 2047, as said below
- coupling: bfloat16 [128, 128, 6, 64, 64], P(('gx', 'gy')), may hold values from -0.25 to 0.25
- send_cluster: int32 [128, 128, 6], P(('gx', 'gy')), may hold values from 0 to 27, as said below
- target_cluster: int32 [128, 128, 6], P(('gx', 'gy')), may hold values from 0 to 28, as said below
Outputs:
- potential: bfloat16 [2048, 256, 64], P(('gx', 'gy'))
The draws below stay inside these ranges and needn't reach their ends.
Inputs may be any that keep to these rules, and one draw needn't show every extreme that they name: `near_source`: leaf l's first source is l itself; the others are distinct offsets o with 0 < |o| <= 8, giving leaf l + o clipped to the range of leaves. send_cluster[p, d, c] is a cluster of device p in the numbering of the steps, on the same level as target_cluster[d, p, c] when that slot is used. target_cluster[d, p, c] is the cluster of device d that receives the slot; the value 28 marks an empty slot. Between devices whose indices differ by at most one all 6 slots are used.
All inputs are finite; a program needn't handle non-finite values.
Results may differ from the reference program's by a relative error of at most 0.0055.
Values may be sent and summed in bfloat16 or wider, within the bound.
No kernel may reach another device: no remote copies, remote signals or barrier semaphores. Data moves between devices by JAX's collectives and lax.ppermute only.
A program may use at most 192 MiB of HBM per device.

```python
import jax
import jax.numpy as jnp
from jax import lax

LEAF = 256
K = 64
R = 64
NEAR = 6
CAP = 6
LEVELS = 3
L_DEV = 16
CLD = 28
CLO = 24
NL = 2048
DEVICES = 128


def far_plan(key):
    shape = (DEVICES, DEVICES, CAP)
    keys = jax.random.split(jax.random.fold_in(key, 7), 4)
    depth = jax.random.randint(keys[0], shape, 0, LEVELS)
    table = []
    offset = 0
    for level_index in range(LEVELS):
        table.append(offset)
        offset = offset + (L_DEV >> level_index)
    starts = jnp.array(table, dtype=jnp.int32)[depth]
    members = jnp.right_shift(jnp.int32(L_DEV), depth)
    source = starts + jax.random.randint(keys[1], shape, 0, 1 << 20) % members
    target = starts + jax.random.randint(keys[2], shape, 0, 1 << 20) % members
    indices = jnp.arange(DEVICES)
    distance = jnp.abs(indices[:, None] - indices[None, :])[:, :, None]
    live = (distance <= 1) | (jax.random.randint(keys[3], shape, 0, 100) < 45)
    target = jnp.where(live, target, CLD)
    return (source.astype(jnp.int32), target.astype(jnp.int32))


def draw_send_cluster(key, part):
    source, target = far_plan(key)
    return jnp.transpose(source, (1, 0, 2))


def draw_target_cluster(key, part):
    source, target = far_plan(key)
    return target


def draw_near_source(key, part):
    total = L_DEV * DEVICES
    reach = L_DEV // 2
    offsets = jnp.concatenate([jnp.arange(-reach, 0), jnp.arange(1, reach + 1)]).astype(jnp.int32)
    scores = jax.random.randint(jax.random.fold_in(key, 11), (total, 2 * reach), 0, 1 << 20) * (2 * reach) + jnp.arange(2 * reach)[None, :]
    order = jnp.argsort(scores, axis=1)
    chosen = offsets[order[:, :NEAR - 1]]
    itself = jnp.arange(total, dtype=jnp.int32)[:, None]
    others = jnp.clip(itself + chosen, 0, total - 1)
    return jnp.concatenate([itself, others], axis=1).astype(jnp.int32)


def block_scale(rng, dims, shards, low, high):
    def one(axis_at, parts):
        heights = jax.random.uniform(jax.random.fold_in(jax.random.fold_in(rng, 6), axis_at), (parts,), jnp.float32, low / len(shards), high / len(shards))
        return jnp.repeat(jnp.exp(heights), dims[axis_at] // parts).reshape((-1,) + (1,) * (len(dims) - axis_at - 1))

    loudness = one(*shards[0])
    for cut in shards[1:]:
        loudness = loudness * one(*cut)
    return loudness


def gaussian(own_key, extent, deviation, bound, cuts=(), held_as=jnp.bfloat16):
    values = jax.random.normal(own_key, extent, jnp.float32) * deviation
    if len(cuts) > 0:
        values = block_scale(own_key, extent, cuts, -0.22, 0.18) * values
    return jnp.clip(values, min=-bound, max=bound).astype(held_as)


def setup_inputs(seed: int = 0) -> dict:
    streams_of = jax.random.split(jax.random.key(seed), 9)
    charges = gaussian(streams_of[0], (NL, LEAF, R), 1.0, 6.0, ((0, 128),))
    leaf_basis = gaussian(streams_of[1], (NL, LEAF, K), LEAF ** -0.5, 0.375, ((0, 128),))
    transfer = gaussian(streams_of[2], (DEVICES, CLO, K, K), (2 * K) ** -0.5, 0.5, ((0, 128),))
    near_blocks = gaussian(streams_of[3], (NL, NEAR, LEAF, LEAF), (LEAF * NEAR) ** -0.5, 0.15625, ((0, 128),))
    near_source = draw_near_source(jax.random.fold_in(streams_of[8], 71), 0)
    coupling = gaussian(streams_of[5], (DEVICES, DEVICES, CAP, K, K), (8 * K) ** -0.5, 0.25, ((0, 128),))
    send_cluster = draw_send_cluster(jax.random.fold_in(streams_of[8], 71), 0)
    target_cluster = draw_target_cluster(jax.random.fold_in(streams_of[8], 71), 0)
    return dict(charges=charges, leaf_basis=leaf_basis, transfer=transfer, near_blocks=near_blocks, near_source=near_source, coupling=coupling, send_cluster=send_cluster, target_cluster=target_cluster)


def reference(charges, leaf_basis, transfer, near_blocks, near_source, coupling, send_cluster, target_cluster):
    highest = lax.Precision.HIGHEST
    single = jnp.float32
    device_count = send_cluster.shape[0]
    columns = charges.reshape(device_count, L_DEV, LEAF, R)
    basis = leaf_basis.reshape(device_count, L_DEV, LEAF, K)
    first_level = jnp.einsum('nlpk,nlpr->nlkr', basis.astype(single), columns.astype(single), precision=highest)
    levels = [first_level.astype(jnp.bfloat16)]
    bounds = []
    offset = 0
    for depth in range(LEVELS - 1):
        members = L_DEV >> depth
        bounds.append((offset, members))
        matrices = transfer[:, offset:offset + members].astype(single)
        lifted = jnp.einsum('nckj,nckr->ncjr', matrices, levels[-1].astype(single), precision=highest)
        levels.append(lifted.reshape(device_count, members // 2, 2, K, R).sum(axis=2).astype(jnp.bfloat16))
        offset = offset + members
    bounds.append((offset, L_DEV >> (LEVELS - 1)))
    upward = jnp.concatenate(levels, axis=1)
    peer_rows = jnp.arange(device_count)[:, None]

    def far_one(device):
        picked = upward[peer_rows, send_cluster[:, device, :]]
        products = jnp.einsum('pckj,pcjr->pckr', coupling[device].astype(single), picked.astype(single), precision=highest)
        summed = jax.ops.segment_sum(products.reshape(device_count * CAP, K, R), target_cluster[device].reshape(-1), num_segments=CLD + 1)
        return summed[:CLD]

    far_field = lax.map(far_one, jnp.arange(device_count))
    down = [far_field[:, lo:lo + size] for lo, size in bounds]
    for depth in range(LEVELS - 2, -1, -1):
        lo, size = bounds[depth]
        spread = jnp.repeat(down[depth + 1], 2, axis=1)
        matrices = transfer[:, lo:lo + size].astype(single)
        down[depth] = down[depth] + jnp.einsum('nckj,ncjr->nckr', matrices, spread, precision=highest)
    far_leaf = jnp.einsum('nlpk,nlkr->nlpr', basis.astype(single), down[0], precision=highest)

    def near_one(pair):
        blocks, sources = pair
        fetched = charges[sources]
        return jnp.einsum('lspq,lsqr->lpr', blocks.astype(single), fetched.astype(single), precision=highest)

    near_field = lax.map(near_one, (near_blocks.reshape(device_count, L_DEV, NEAR, LEAF, LEAF), near_source.reshape(device_count, L_DEV, NEAR)))
    return (near_field + far_leaf).astype(jnp.bfloat16).reshape(NL, LEAF, R)
```

```python
import functools

import jax
import jax.numpy as jnp
from jax import lax
from jax.experimental import pallas as pl
from jax.experimental.pallas import tpu as pltpu
from jax.sharding import PartitionSpec as P

AXES = ("gx", "gy")
LEVELS = 3
F32 = jnp.float32
BF16 = jnp.bfloat16


def level_bounds(leaves):
    bounds, offset = [], 0
    for depth in range(LEVELS):
        bounds.append((offset, leaves >> depth))
        offset += leaves >> depth
    return bounds, offset


def contract(a, b, da, db):
    return lax.dot_general(a, b, (((da,), (db,)), ((), ())), preferred_element_type=F32)


def split_pair(x):
    high = x.astype(BF16)
    return high, (x - high.astype(F32)).astype(BF16)


def up_kernel(bounds, slots, per_step, send, charges, basis, transfer, out, upward):
    half = upward.shape[1]
    step = pl.program_id(0)

    @pl.when(step == 0)
    def _():
        def put(c, block):
            block = block.astype(BF16)
            upward[c] = jnp.concatenate([block[:half], block[half:]], axis=1)
            return block

        held = []
        for leaf in range(bounds[0][1]):
            held.append(put(leaf, contract(basis[leaf], charges[leaf], 1, 1)))
        for depth in range(LEVELS - 1):
            lo, size = bounds[depth]
            above = bounds[depth + 1][0]
            parents = []
            for c in range(size // 2):
                both = jnp.concatenate([transfer[lo + 2 * c], transfer[lo + 2 * c + 1]], axis=0)
                kids = jnp.concatenate([held[2 * c], held[2 * c + 1]], axis=0)
                parents.append(put(above + c, contract(both, kids, 0, 0)))
            held = parents

    def copy(i, carry):
        d = step * per_step + i
        for c in range(slots):
            out[pl.ds((i * slots + c) * half, half), :] = upward[send[c, d]]
        return carry

    lax.fori_loop(0, per_step, copy, 0, unroll=4)


def near_kernel(first, source, low, own, high, blocks, out, window):
    leaf = pl.program_id(0)
    reach, leaves = low.shape[0], own.shape[0]

    @pl.when(leaf == 0)
    def _():
        window[pl.ds(0, reach)] = low[...]
        window[pl.ds(reach, leaves)] = own[...]
        window[pl.ds(reach + leaves, reach)] = high[...]

    total = None
    for s in range(blocks.shape[1]):
        row = source[s, leaf] - first[0] + reach
        term = contract(window[row], blocks[0, s], 1, 1)
        total = term if total is None else total + term
    out[0] = total


def far_kernel(bounds, slots, peers, target, coupling, fetched, basis, transfer, near, out, acc):
    half = 32
    step = pl.program_id(0)

    @pl.when(step == 0)
    def _():
        acc[...] = jnp.zeros_like(acc)

    for i in range(peers):
        for c in range(slots):
            v = fetched[pl.ds((i * slots + c) * half, half), :]
            u = jnp.concatenate([v, pltpu.roll(v, 64, 1)], axis=0)
            product = contract(coupling[i, c], u, 1, 0)
            acc[target[c, step * peers + i]] += product

    @pl.when(step == pl.num_programs(0) - 1)
    def _():
        rank = basis.shape[1]
        down = [acc[c][:, :rank] for c in range(bounds[-1][0] + bounds[-1][1])]
        for depth in range(LEVELS - 2, -1, -1):
            lo, size = bounds[depth]
            above = bounds[depth + 1][0]
            for c in range(size):
                high, low = split_pair(down[above + c // 2])
                matrix = transfer[lo + c]
                down[lo + c] = down[lo + c] + contract(matrix, high, 1, 0) + contract(matrix, low, 1, 0)
        for leaf in range(bounds[0][1]):
            high, low = split_pair(down[leaf])
            far_leaf = contract(high, basis[leaf], 0, 0) + contract(low, basis[leaf], 0, 0)
            out[leaf] = (near[leaf] + far_leaf).astype(BF16)


def whole(shape):
    return pl.BlockSpec(shape, lambda *_: (0,) * len(shape))


def shards(
    charges, leaf_basis, transfer, near_blocks, near_source, coupling, send_cluster, target_cluster
):
    leaves, panels, width = charges.shape
    rank = leaf_basis.shape[2]
    peers, slots = send_cluster.shape[1:]
    near = near_source.shape[1]
    bounds, clusters = level_bounds(leaves)
    half = rank * width // 128
    reach = leaves // 2
    outer, inner = lax.axis_size("gx"), lax.axis_size("gy")
    count = outer * inner

    charges_t = jnp.swapaxes(charges, 1, 2)
    basis_t = jnp.swapaxes(leaf_basis, 1, 2)
    matrices = transfer[0]
    send = jnp.transpose(send_cluster[0], (1, 0))
    target = jnp.transpose(target_cluster[0], (1, 0))
    source = jnp.transpose(near_source, (1, 0))

    up = [(i, i + 1) for i in range(count - 1)]
    low = lax.ppermute(charges_t[leaves - reach :], AXES, up)
    high = lax.ppermute(charges_t[:reach], AXES, [(b, a) for a, b in up])

    steps = 8
    per_step = peers // steps
    packed = pl.pallas_call(
        functools.partial(up_kernel, bounds, slots, per_step),
        grid_spec=pltpu.PrefetchScalarGridSpec(
            num_scalar_prefetch=1,
            grid=(steps,),
            in_specs=[
                whole((leaves, width, panels)),
                whole((leaves, rank, panels)),
                whole(matrices.shape),
            ],
            out_specs=pl.BlockSpec((per_step * slots * half, 128), lambda i, *_: (i, 0)),
            scratch_shapes=[pltpu.VMEM((clusters, half, 128), BF16)],
        ),
        out_shape=jax.ShapeDtypeStruct((peers * slots * half, 128), BF16),
        name="up_pick",
    )(send, charges_t, basis_t, matrices)

    packed, low, high = lax.optimization_barrier((packed, low, high))
    fetched = lax.all_to_all(packed, AXES, split_axis=0, concat_axis=0, tiled=True)

    first = (lax.axis_index(AXES) * leaves).reshape(1)
    near_field = pl.pallas_call(
        near_kernel,
        grid_spec=pltpu.PrefetchScalarGridSpec(
            num_scalar_prefetch=2,
            grid=(leaves,),
            in_specs=[
                whole((reach, width, panels)),
                whole((leaves, width, panels)),
                whole((reach, width, panels)),
                pl.BlockSpec((1, near, panels, panels), lambda i, *_: (i, 0, 0, 0)),
            ],
            out_specs=pl.BlockSpec((1, width, panels), lambda i, *_: (i, 0, 0)),
            scratch_shapes=[pltpu.VMEM((leaves + 2 * reach, width, panels), BF16)],
        ),
        out_shape=jax.ShapeDtypeStruct((leaves, width, panels), F32),
        cost_estimate=pl.CostEstimate(
            flops=2 * leaves * near * panels * panels * width,
            bytes_accessed=2 * leaves * near * panels * panels,
            transcendentals=0,
        ),
        name="near",
    )(first, source, low, charges_t, high, near_blocks)

    fsteps = 16
    fpeers = peers // fsteps
    potential_t = pl.pallas_call(
        functools.partial(far_kernel, bounds, slots, fpeers),
        grid_spec=pltpu.PrefetchScalarGridSpec(
            num_scalar_prefetch=1,
            grid=(fsteps,),
            in_specs=[
                pl.BlockSpec((fpeers, slots, rank, rank), lambda i, *_: (i, 0, 0, 0)),
                pl.BlockSpec((fpeers * slots * half, 128), lambda i, *_: (i, 0)),
                whole((leaves, rank, panels)),
                whole(matrices.shape),
                whole((leaves, width, panels)),
            ],
            out_specs=whole((leaves, width, panels)),
            scratch_shapes=[pltpu.VMEM((clusters + 1, rank, 128), F32)],
        ),
        out_shape=jax.ShapeDtypeStruct((leaves, width, panels), BF16),
        name="far",
    )(target, coupling[0], fetched, basis_t, matrices, near_field)
    return jnp.swapaxes(potential_t, 1, 2)


def solution(mesh):
    placed = (
        P(AXES, None, None),
        P(AXES, None, None),
        P(AXES, None, None, None),
        P(AXES, None, None, None),
        P(AXES, None),
        P(AXES, None, None, None, None),
        P(AXES, None, None),
        P(AXES, None, None),
    )
    return jax.shard_map(
        shards, mesh=mesh, in_specs=placed, out_specs=P(AXES, None, None), check_vma=False
    )
```

```python
import functools

import jax
import jax.numpy as jnp
from jax import lax
from jax.experimental import pallas as pl
from jax.experimental.pallas import tpu as pltpu
from jax.sharding import PartitionSpec as P

AXES = ("gx", "gy")
LEVELS = 3
F32 = jnp.float32
BF16 = jnp.bfloat16


def level_bounds(leaves):
    bounds, offset = [], 0
    for depth in range(LEVELS):
        bounds.append((offset, leaves >> depth))
        offset += leaves >> depth
    return bounds, offset


def contract(a, b, da, db):
    return lax.dot_general(a, b, (((da,), (db,)), ((), ())), preferred_element_type=F32)


def split_pair(x):
    high = x.astype(BF16)
    return high, (x - high.astype(F32)).astype(BF16)


def up_kernel(bounds, slots, send, charges, basis, transfer, out, upward, staged, sems):
    half = upward.shape[1]
    chunks, rows = staged.shape[:2]
    per_chunk = rows // (slots * half)

    def put(c, block):
        block = block.astype(BF16)
        upward[c] = jnp.concatenate([block[:half], block[half:]], axis=1)
        return block

    held = []
    for leaf in range(bounds[0][1]):
        held.append(put(leaf, contract(basis[leaf], charges[leaf], 1, 1)))
    for depth in range(LEVELS - 1):
        lo, size = bounds[depth]
        above = bounds[depth + 1][0]
        parents = []
        for c in range(size // 2):
            both = jnp.concatenate([transfer[lo + 2 * c], transfer[lo + 2 * c + 1]], axis=0)
            kids = jnp.concatenate([held[2 * c], held[2 * c + 1]], axis=0)
            parents.append(put(above + c, contract(both, kids, 0, 0)))
        held = parents

    def send_out(j):
        rows_out = out.at[pl.ds(pl.multiple_of(j * rows, rows), rows)]
        return pltpu.make_async_copy(staged.at[j], rows_out, sems.at[j])

    @pl.loop(0, chunks)
    def _(j):
        def copy(i, carry):
            for c in range(slots):
                at = pl.multiple_of((i * slots + c) * half, half)
                staged[j, pl.ds(at, half), :] = upward[send[c, 0, j * per_chunk + i]]
            return carry

        lax.fori_loop(0, per_chunk, copy, 0, unroll=4)
        send_out(j).start()

    @pl.loop(0, chunks)
    def _(j):
        send_out(j).wait()


def near_kernel(first, source, low, own, high, blocks, out, window):
    step = pl.program_id(0)
    reach, leaves = low.shape[0], own.shape[0]
    per_step, near = blocks.shape[:2]

    @pl.when(step == 0)
    def _():
        window[pl.ds(0, reach)] = low[...]
        window[pl.ds(reach, leaves)] = own[...]
        window[pl.ds(reach + leaves, reach)] = high[...]

    for i in range(per_step):
        total = None
        for s in range(near):
            row = source[s, step * per_step + i] - first[0] + reach
            term = contract(window[row], blocks[i, s], 1, 1)
            total = term if total is None else total + term
        out[i] = total


def far_kernel(
    bounds, slots, chunks, target, coupling, fetched, basis, transfer, near, out,
    cbuf, fbuf, bbuf, tbuf, nbuf, acc, csem, fsem, esem,
):
    peers = cbuf.shape[0] // chunks
    half = fbuf.shape[0] // (cbuf.shape[0] * slots)
    rows = peers * slots * half

    def fetch(j):
        some = pl.ds(pl.multiple_of(j * peers, peers), peers)
        some_rows = pl.ds(pl.multiple_of(j * rows, rows), rows)
        return (
            pltpu.make_async_copy(coupling.at[some], cbuf.at[some], csem.at[j]),
            pltpu.make_async_copy(fetched.at[some_rows], fbuf.at[some_rows], fsem.at[j]),
        )

    extra = [
        pltpu.make_async_copy(source, held, esem.at[i])
        for i, (source, held) in enumerate(((transfer, tbuf), (basis, bbuf), (near, nbuf)))
    ]

    @pl.loop(0, chunks)
    def _(j):
        for copy in fetch(j):
            copy.start()

    for copy in extra:
        copy.start()
    acc[...] = jnp.zeros_like(acc)

    @pl.loop(0, chunks)
    def _(j):
        for copy in fetch(j):
            copy.wait()
        for i in range(peers):
            p = j * peers + i
            for c in range(slots):
                at = pl.multiple_of((p * slots + c) * half, half)
                v = fbuf[pl.ds(at, half), :]
                u = jnp.concatenate([v, pltpu.roll(v, 64, 1)], axis=0)
                acc[target[c, 0, p]] += contract(cbuf[p, c], u, 1, 0)

    for copy in extra:
        copy.wait()
    rank = bbuf.shape[1]
    down = [acc[c][:, :rank] for c in range(bounds[-1][0] + bounds[-1][1])]
    for depth in range(LEVELS - 2, -1, -1):
        lo, size = bounds[depth]
        above = bounds[depth + 1][0]
        for c in range(size):
            high, low = split_pair(down[above + c // 2])
            matrix = tbuf[lo + c]
            down[lo + c] = down[lo + c] + contract(matrix, high, 1, 0) + contract(matrix, low, 1, 0)
    for leaf in range(bounds[0][1]):
        high, low = split_pair(down[leaf])
        far_leaf = contract(high, bbuf[leaf], 0, 0) + contract(low, bbuf[leaf], 0, 0)
        out[leaf] = (nbuf[leaf] + far_leaf).astype(BF16)


def whole(shape):
    return pl.BlockSpec(shape, lambda *_: (0,) * len(shape))


def shards(
    charges, leaf_basis, transfer, near_blocks, near_source, coupling, send_cluster, target_cluster
):
    leaves, panels, width = charges.shape
    rank = leaf_basis.shape[2]
    peers, slots = send_cluster.shape[1:]
    near = near_source.shape[1]
    bounds, clusters = level_bounds(leaves)
    half = rank * width // 128
    reach = leaves // 2
    outer, inner = lax.axis_size("gx"), lax.axis_size("gy")
    count = outer * inner

    charges_t = jnp.swapaxes(charges, 1, 2)
    basis_t = jnp.swapaxes(leaf_basis, 1, 2)
    matrices = transfer[0]
    send = jnp.transpose(send_cluster, (2, 0, 1))
    target = jnp.transpose(target_cluster, (2, 0, 1))
    source = jnp.transpose(near_source, (1, 0))

    up = [(i, i + 1) for i in range(count - 1)]
    low = lax.ppermute(charges_t[leaves - reach :], AXES, up)
    high = lax.ppermute(charges_t[:reach], AXES, [(b, a) for a, b in up])

    chunks = 8
    packed = pl.pallas_call(
        functools.partial(up_kernel, bounds, slots),
        grid_spec=pltpu.PrefetchScalarGridSpec(
            num_scalar_prefetch=1,
            grid=(),
            in_specs=[pl.BlockSpec(memory_space=pltpu.VMEM)] * 3,
            out_specs=pl.BlockSpec(memory_space=pl.ANY),
            scratch_shapes=[
                pltpu.VMEM((clusters, half, 128), BF16),
                pltpu.VMEM((chunks, peers * slots * half // chunks, 128), BF16),
                pltpu.SemaphoreType.DMA((chunks,)),
            ],
        ),
        out_shape=jax.ShapeDtypeStruct((peers * slots * half, 128), BF16),
        cost_estimate=pl.CostEstimate(
            flops=2 * leaves * panels * rank * width,
            bytes_accessed=2 * peers * slots * rank * width,
            transcendentals=0,
        ),
        name="up_pick",
    )(send, charges_t, basis_t, matrices)

    packed, low, high = lax.optimization_barrier((packed, low, high))
    fetched = lax.all_to_all(packed, AXES, split_axis=0, concat_axis=0, tiled=True)

    per_step = 4
    first = (lax.axis_index(AXES) * leaves).reshape(1)
    near_field = pl.pallas_call(
        near_kernel,
        grid_spec=pltpu.PrefetchScalarGridSpec(
            num_scalar_prefetch=2,
            grid=(leaves // per_step,),
            in_specs=[
                whole((reach, width, panels)),
                whole((leaves, width, panels)),
                whole((reach, width, panels)),
                pl.BlockSpec((per_step, near, panels, panels), lambda i, *_: (i, 0, 0, 0)),
            ],
            out_specs=pl.BlockSpec((per_step, width, panels), lambda i, *_: (i, 0, 0)),
            scratch_shapes=[pltpu.VMEM((leaves + 2 * reach, width, panels), BF16)],
        ),
        out_shape=jax.ShapeDtypeStruct((leaves, width, panels), F32),
        cost_estimate=pl.CostEstimate(
            flops=2 * leaves * near * panels * panels * width,
            bytes_accessed=2 * leaves * near * panels * panels,
            transcendentals=0,
        ),
        name="near",
    )(first, source, low, charges_t, high, near_blocks)

    fchunks = 16
    potential_t = pl.pallas_call(
        functools.partial(far_kernel, bounds, slots, fchunks),
        grid_spec=pltpu.PrefetchScalarGridSpec(
            num_scalar_prefetch=1,
            grid=(),
            in_specs=[pl.BlockSpec(memory_space=pl.ANY)] * 5,
            out_specs=pl.BlockSpec(memory_space=pltpu.VMEM),
            scratch_shapes=[
                pltpu.VMEM((peers, slots, rank, rank), BF16),
                pltpu.VMEM((peers * slots * half, 128), BF16),
                pltpu.VMEM((leaves, rank, panels), BF16),
                pltpu.VMEM(matrices.shape, BF16),
                pltpu.VMEM((leaves, width, panels), F32),
                pltpu.VMEM((clusters + 1, rank, 128), F32),
                pltpu.SemaphoreType.DMA((fchunks,)),
                pltpu.SemaphoreType.DMA((fchunks,)),
                pltpu.SemaphoreType.DMA((3,)),
            ],
        ),
        out_shape=jax.ShapeDtypeStruct((leaves, width, panels), BF16),
        name="far",
    )(target, coupling[0], fetched, basis_t, matrices, near_field)
    return jnp.swapaxes(potential_t, 1, 2)


def solution(mesh):
    placed = (
        P(AXES, None, None),
        P(AXES, None, None),
        P(AXES, None, None, None),
        P(AXES, None, None, None),
        P(AXES, None),
        P(AXES, None, None, None, None),
        P(AXES, None, None),
        P(AXES, None, None),
    )
    return jax.shard_map(
        shards, mesh=mesh, in_specs=placed, out_specs=P(AXES, None, None), check_vma=False
    )
```

```python
import functools

import jax
import jax.numpy as jnp
from jax import lax
from jax.experimental import pallas as pl
from jax.experimental.pallas import tpu as pltpu
from jax.sharding import PartitionSpec as P

AXES = ("gx", "gy")
LEVELS = 3
F32 = jnp.float32
BF16 = jnp.bfloat16


def level_bounds(leaves):
    bounds, offset = [], 0
    for depth in range(LEVELS):
        bounds.append((offset, leaves >> depth))
        offset += leaves >> depth
    return bounds, offset


def contract(a, b, da, db):
    return lax.dot_general(a, b, (((da,), (db,)), ((), ())), preferred_element_type=F32)


def split_pair(x):
    high = x.astype(BF16)
    return high, (x - high.astype(F32)).astype(BF16)


def left_lanes(shape):
    return lax.broadcasted_iota(jnp.int32, shape, 1) < shape[1] // 2


def up_kernel(bounds, slots, send, charges, basis, transfer, out, upward, staged, sems):
    rank = upward.shape[1]
    chunks, rows = staged.shape[:2]
    pairs = slots // 2
    per_chunk = rows // (pairs * rank)

    def put(c, block):
        block = block.astype(BF16)
        upward[c] = jnp.concatenate([block, block], axis=1)
        return block

    held = []
    for leaf in range(bounds[0][1]):
        held.append(put(leaf, contract(basis[leaf], charges[leaf], 1, 1)))
    for depth in range(LEVELS - 1):
        lo, size = bounds[depth]
        above = bounds[depth + 1][0]
        parents = []
        for c in range(size // 2):
            both = jnp.concatenate([transfer[lo + 2 * c], transfer[lo + 2 * c + 1]], axis=0)
            kids = jnp.concatenate([held[2 * c], held[2 * c + 1]], axis=0)
            parents.append(put(above + c, contract(both, kids, 0, 0)))
        held = parents

    def send_out(j):
        rows_out = out.at[pl.ds(pl.multiple_of(j * rows, rows), rows)]
        return pltpu.make_async_copy(staged.at[j], rows_out, sems.at[j])

    left = left_lanes(upward.shape[1:])

    @pl.loop(0, chunks)
    def _(j):
        def copy(i, carry):
            d = j * per_chunk + i
            for q in range(pairs):
                at = pl.multiple_of((i * pairs + q) * rank, rank)
                even, odd = upward[send[2 * q, 0, d]], upward[send[2 * q + 1, 0, d]]
                staged[j, pl.ds(at, rank), :] = jnp.where(left, even, odd)
            return carry

        lax.fori_loop(0, per_chunk, copy, 0, unroll=4)
        send_out(j).start()

    @pl.loop(0, chunks)
    def _(j):
        send_out(j).wait()


def near_kernel(first, source, low, own, high, blocks, out, window):
    step = pl.program_id(0)
    reach, leaves = low.shape[0], own.shape[0]
    per_step, near = blocks.shape[:2]

    @pl.when(step == 0)
    def _():
        window[pl.ds(0, reach)] = low[...]
        window[pl.ds(reach, leaves)] = own[...]
        window[pl.ds(reach + leaves, reach)] = high[...]

    for i in range(per_step):
        total = None
        for s in range(near):
            row = source[s, step * per_step + i] - first[0] + reach
            term = contract(window[row], blocks[i, s], 1, 1)
            total = term if total is None else total + term
        out[i] = total


def far_kernel(
    bounds, chunks, target, coupling, fetched, basis, transfer, near, out,
    cbuf, fbuf, bbuf, tbuf, nbuf, acc0, acc1, acc2, acc3, csem, fsem, esem,
):
    count, pairs, rank, lanes = coupling.shape
    peers = count // chunks
    rows = peers * pairs * rank

    def fetch(j):
        some = pl.ds(pl.multiple_of(j * peers, peers), peers)
        some_rows = pl.ds(pl.multiple_of(j * rows, rows), rows)
        return (
            pltpu.make_async_copy(fetched.at[some_rows], fbuf.at[some_rows], fsem.at[j]),
            pltpu.make_async_copy(coupling.at[some], cbuf.at[some], csem.at[j]),
        )

    extra = [
        pltpu.make_async_copy(source, held, esem.at[i])
        for i, (source, held) in enumerate(((transfer, tbuf), (basis, bbuf), (near, nbuf)))
    ]

    @pl.loop(0, chunks)
    def _(j):
        for copy in fetch(j):
            copy.start()

    for copy in extra:
        copy.start()
    evens, odds = (acc0, acc1), (acc2, acc3)
    for acc in evens + odds:
        acc[...] = jnp.zeros_like(acc)
    left = left_lanes((rank, lanes))
    side = lanes // 2

    @pl.loop(0, chunks)
    def _(j):
        for copy in fetch(j):
            copy.wait()
        for i in range(peers):
            p = j * peers + i
            for q in range(pairs):
                v = fbuf[pl.ds(pl.multiple_of((p * pairs + q) * rank, rank), rank), :]
                zero = jnp.zeros_like(v)
                u = jnp.concatenate([jnp.where(left, v, zero), jnp.where(left, zero, v)], axis=0)
                product = contract(cbuf[p, q], u, 1, 0)
                turn = (i * pairs + q) % len(evens)
                evens[turn][target[2 * q, 0, p]] += product
                odds[turn][target[2 * q + 1, 0, p]] += product

    for copy in extra:
        copy.wait()

    def both_sides(x):
        return (x + pltpu.roll(x, side, 1))[:, :side]

    down = []
    for c in range(bounds[-1][0] + bounds[-1][1]):
        even = sum(acc[c] for acc in evens)
        odd = sum(acc[c] for acc in odds)
        down.append(both_sides(jnp.where(left, even, odd)))
    for depth in range(LEVELS - 2, -1, -1):
        lo, size = bounds[depth]
        above = bounds[depth + 1][0]
        for c in range(size):
            parent = jnp.concatenate(split_pair(down[above + c // 2]), axis=1)
            down[lo + c] = down[lo + c] + both_sides(contract(tbuf[lo + c], parent, 1, 0))
    for leaf in range(bounds[0][1]):
        block = bbuf[leaf]
        far_leaf = contract(
            jnp.concatenate(split_pair(down[leaf]), axis=0),
            jnp.concatenate([block, block], axis=0),
            0,
            0,
        )
        out[leaf] = (nbuf[leaf] + far_leaf).astype(BF16)


def far_call(bounds, target, coupled, fetched, basis, transfer, near, chunks=8, flags=None):
    peers, pairs, rank, lanes = coupled.shape
    clusters = bounds[-1][0] + bounds[-1][1]
    return pl.pallas_call(
        functools.partial(far_kernel, bounds, chunks),
        grid_spec=pltpu.PrefetchScalarGridSpec(
            num_scalar_prefetch=1,
            grid=(),
            in_specs=[pl.BlockSpec(memory_space=pl.ANY)] * 5,
            out_specs=pl.BlockSpec(memory_space=pltpu.VMEM),
            scratch_shapes=[
                pltpu.VMEM(coupled.shape, BF16),
                pltpu.VMEM(fetched.shape, BF16),
                pltpu.VMEM(basis.shape, BF16),
                pltpu.VMEM(transfer.shape, BF16),
                pltpu.VMEM(near.shape, F32),
                *[pltpu.VMEM((clusters + 1, rank, lanes), F32)] * 4,
                pltpu.SemaphoreType.DMA((chunks,)),
                pltpu.SemaphoreType.DMA((chunks,)),
                pltpu.SemaphoreType.DMA((3,)),
            ],
        ),
        out_shape=jax.ShapeDtypeStruct(near.shape, BF16),
        compiler_params=pltpu.CompilerParams(flags=flags or {}),
        name="far",
    )(target, coupled, fetched, basis, transfer, near)


def whole(shape):
    return pl.BlockSpec(shape, lambda *_: (0,) * len(shape))


def shards(
    charges, leaf_basis, transfer, near_blocks, near_source, coupling, send_cluster, target_cluster
):
    leaves, panels, width = charges.shape
    rank = leaf_basis.shape[2]
    peers, slots = send_cluster.shape[1:]
    near = near_source.shape[1]
    bounds, clusters = level_bounds(leaves)
    pairs = slots // 2
    lanes = 2 * width
    coupled = coupling[0].reshape(peers, pairs, 2, rank, rank)
    coupled = jnp.swapaxes(coupled, 2, 3).reshape(peers, pairs, rank, 2 * rank)
    reach = leaves // 2
    outer, inner = lax.axis_size("gx"), lax.axis_size("gy")
    count = outer * inner

    charges_t = jnp.swapaxes(charges, 1, 2)
    basis_t = jnp.swapaxes(leaf_basis, 1, 2)
    matrices = transfer[0]
    send = jnp.transpose(send_cluster, (2, 0, 1))
    target = jnp.transpose(target_cluster, (2, 0, 1))
    source = jnp.transpose(near_source, (1, 0))

    up = [(i, i + 1) for i in range(count - 1)]
    low = lax.ppermute(charges_t[leaves - reach :], AXES, up)
    high = lax.ppermute(charges_t[:reach], AXES, [(b, a) for a, b in up])

    chunks = 8
    packed = pl.pallas_call(
        functools.partial(up_kernel, bounds, slots),
        grid_spec=pltpu.PrefetchScalarGridSpec(
            num_scalar_prefetch=1,
            grid=(),
            in_specs=[pl.BlockSpec(memory_space=pltpu.VMEM)] * 3,
            out_specs=pl.BlockSpec(memory_space=pl.ANY),
            scratch_shapes=[
                pltpu.VMEM((clusters, rank, lanes), BF16),
                pltpu.VMEM((chunks, peers * pairs * rank // chunks, lanes), BF16),
                pltpu.SemaphoreType.DMA((chunks,)),
            ],
        ),
        out_shape=jax.ShapeDtypeStruct((peers * pairs * rank, lanes), BF16),
        cost_estimate=pl.CostEstimate(
            flops=2 * leaves * panels * rank * width,
            bytes_accessed=2 * peers * slots * rank * width,
            transcendentals=0,
        ),
        name="up_pick",
    )(send, charges_t, basis_t, matrices)

    packed, low, high = lax.optimization_barrier((packed, low, high))
    fetched = lax.all_to_all(packed, AXES, split_axis=0, concat_axis=0, tiled=True)

    per_step = 4
    first = (lax.axis_index(AXES) * leaves).reshape(1)
    near_field = pl.pallas_call(
        near_kernel,
        grid_spec=pltpu.PrefetchScalarGridSpec(
            num_scalar_prefetch=2,
            grid=(leaves // per_step,),
            in_specs=[
                whole((reach, width, panels)),
                whole((leaves, width, panels)),
                whole((reach, width, panels)),
                pl.BlockSpec((per_step, near, panels, panels), lambda i, *_: (i, 0, 0, 0)),
            ],
            out_specs=pl.BlockSpec((per_step, width, panels), lambda i, *_: (i, 0, 0)),
            scratch_shapes=[pltpu.VMEM((leaves + 2 * reach, width, panels), BF16)],
        ),
        out_shape=jax.ShapeDtypeStruct((leaves, width, panels), F32),
        cost_estimate=pl.CostEstimate(
            flops=2 * leaves * near * panels * panels * width,
            bytes_accessed=2 * leaves * near * panels * panels,
            transcendentals=0,
        ),
        compiler_params=pltpu.CompilerParams(vmem_limit_bytes=24 << 20),
        name="near",
    )(first, source, low, charges_t, high, near_blocks)

    potential_t = far_call(bounds, target, coupled, fetched, basis_t, matrices, near_field)
    return jnp.swapaxes(potential_t, 1, 2)


def solution(mesh):
    placed = (
        P(AXES, None, None),
        P(AXES, None, None),
        P(AXES, None, None, None),
        P(AXES, None, None, None),
        P(AXES, None),
        P(AXES, None, None, None, None),
        P(AXES, None, None),
        P(AXES, None, None),
    )
    return jax.shard_map(
        shards, mesh=mesh, in_specs=placed, out_specs=P(AXES, None, None), check_vma=False
    )
```

```python
import functools

import jax
import jax.numpy as jnp
from jax import lax
from jax.experimental import pallas as pl
from jax.experimental.pallas import tpu as pltpu
from jax.sharding import PartitionSpec as P

AXES = ("gx", "gy")
LEVELS = 3
GROUP = 4
F32 = jnp.float32
BF16 = jnp.bfloat16


def level_bounds(leaves):
    bounds, offset = [], 0
    for depth in range(LEVELS):
        bounds.append((offset, leaves >> depth))
        offset += leaves >> depth
    return bounds, offset


def contract(a, b, da, db):
    return lax.dot_general(a, b, (((da,), (db,)), ((), ())), preferred_element_type=F32)


def split_pair(x):
    high = x.astype(BF16)
    return high, (x - high.astype(F32)).astype(BF16)


def left_lanes(shape):
    return lax.broadcasted_iota(jnp.int32, shape, 1) < shape[1] // 2


def up_kernel(bounds, slots, send, charges, basis, transfer, out, upward, staged, sems):
    rank = upward.shape[1]
    chunks, rows = staged.shape[:2]
    pairs = slots // 2
    per_chunk = rows // (pairs * rank)

    def put(c, block):
        block = block.astype(BF16)
        upward[c] = jnp.concatenate([block, block], axis=1)
        return block

    held = []
    for leaf in range(bounds[0][1]):
        held.append(put(leaf, contract(basis[leaf], charges[leaf], 1, 1)))
    for depth in range(LEVELS - 1):
        lo, size = bounds[depth]
        above = bounds[depth + 1][0]
        parents = []
        for c in range(size // 2):
            both = jnp.concatenate([transfer[lo + 2 * c], transfer[lo + 2 * c + 1]], axis=0)
            kids = jnp.concatenate([held[2 * c], held[2 * c + 1]], axis=0)
            parents.append(put(above + c, contract(both, kids, 0, 0)))
        held = parents

    def send_out(j):
        rows_out = out.at[pl.ds(pl.multiple_of(j * rows, rows), rows)]
        return pltpu.make_async_copy(staged.at[j], rows_out, sems.at[j])

    left = left_lanes(upward.shape[1:])

    @pl.loop(0, chunks)
    def _(j):
        def copy(i, carry):
            d = j * per_chunk + i
            for q in range(pairs):
                at = pl.multiple_of((i * pairs + q) * rank, rank)
                even, odd = upward[send[2 * q, 0, d]], upward[send[2 * q + 1, 0, d]]
                staged[j, pl.ds(at, rank), :] = jnp.where(left, even, odd)
            return carry

        lax.fori_loop(0, per_chunk, copy, 0, unroll=4)
        send_out(j).start()

    @pl.loop(0, chunks)
    def _(j):
        send_out(j).wait()


def near_kernel(reach, first, source, own, blocks, out, listed, window):
    step = pl.program_id(0)
    leaves = own.shape[0]
    per_step, near = blocks.shape[:2]

    @pl.when(step == 0)
    def _():
        edge = jnp.zeros((reach, *own.shape[1:]), BF16)
        window[pl.ds(0, reach)] = edge
        window[pl.ds(reach, leaves)] = own[...]
        window[pl.ds(reach + leaves, reach)] = edge

        def note(leaf, found):
            for s in range(near):
                row = source[s, leaf] - first[0]
                inside = (row >= 0) & (row < leaves)
                edge_row = jnp.where(row < 0, row + reach, row - leaves + reach)
                listed[found] = edge_row | (s << 8) | (leaf << 16) | (leaf << 24)
                found = found + jnp.where(inside, 0, 1)
            return found

        most = leaves * near + GROUP

        def clear(i, carry):
            listed[i] = leaves << 24
            return carry

        lax.fori_loop(0, most, clear, 0, unroll=GROUP)
        found = lax.fori_loop(0, leaves, note, 0)
        for i in range(GROUP):
            listed[found + i] = leaves << 24
        listed[most] = (found + GROUP - 1) // GROUP

    for i in range(per_step):
        total = None
        for s in range(near):
            row = source[s, step * per_step + i] - first[0] + reach
            term = contract(window[row], blocks[i, s], 1, 1)
            total = term if total is None else total + term
        out[i] = total


def far_kernel(
    bounds, chunks, target, listed, coupling, fetched, basis, transfer, near, low, high, blocks, out,
    cbuf, fbuf, nbuf, acc0, acc1, acc2, acc3, edge, held, csem, fsem, esem, hsem,
):
    count, pairs, rank, lanes = coupling.shape
    peers = count // chunks
    rows = peers * pairs * rank

    def fetch(j):
        some = pl.ds(pl.multiple_of(j * peers, peers), peers)
        some_rows = pl.ds(pl.multiple_of(j * rows, rows), rows)
        return (
            pltpu.make_async_copy(fetched.at[some_rows], fbuf.at[some_rows], fsem.at[j]),
            pltpu.make_async_copy(coupling.at[some], cbuf.at[some], csem.at[j]),
        )

    leaves, reach = near.shape[0], low.shape[0]
    moves = (
        (low, edge.at[pl.ds(0, reach)]),
        (high, edge.at[pl.ds(reach, reach)]),
        (near, nbuf.at[pl.ds(0, leaves)]),
    )
    extra = [pltpu.make_async_copy(a, b, esem.at[i]) for i, (a, b) in enumerate(moves)]
    groups = listed[leaves * blocks.shape[1] + GROUP]

    def fetch_block(i, slot):
        entry = listed[i]
        block = blocks.at[(entry >> 16) & 255, (entry >> 8) & 255]
        return pltpu.make_async_copy(block, held.at[slot], hsem.at[slot])

    def add_blocks(i, slot):
        terms = [contract(edge[listed[i + k] & 255], held[slot + k], 1, 1) for k in range(GROUP)]
        for k in range(GROUP):
            nbuf[listed[i + k] >> 24] += terms[k]

    for copy in extra:
        copy.start()

    @pl.loop(0, chunks)
    def _(j):
        for copy in fetch(j):
            copy.start()
        for k in range(GROUP):
            fetch_block(j * GROUP + k, j * GROUP + k).start()

    evens, odds = (acc0, acc1), (acc2, acc3)
    for acc in evens + odds:
        acc[...] = jnp.zeros_like(acc)
    left = left_lanes((rank, lanes))
    side = lanes // 2
    for copy in extra:
        copy.wait()

    @pl.loop(0, chunks)
    def _(j):
        for copy in fetch(j):
            copy.wait()
        for k in range(GROUP):
            fetch_block(j * GROUP + k, j * GROUP + k).wait()
        add_blocks(j * GROUP, j * GROUP)
        for i in range(peers):
            p = j * peers + i
            for q in range(pairs):
                v = fbuf[pl.ds(pl.multiple_of((p * pairs + q) * rank, rank), rank), :]
                zero = jnp.zeros_like(v)
                u = jnp.concatenate([jnp.where(left, v, zero), jnp.where(left, zero, v)], axis=0)
                product = contract(cbuf[p, q], u, 1, 0)
                turn = (i * pairs + q) % len(evens)
                evens[turn][target[2 * q, 0, p]] += product
                odds[turn][target[2 * q + 1, 0, p]] += product

    @pl.loop(chunks, groups)
    def _(g):
        for k in range(GROUP):
            fetch_block(g * GROUP + k, k).start()
        for k in range(GROUP):
            fetch_block(g * GROUP + k, k).wait()
        add_blocks(g * GROUP, 0)

    def both_sides(x):
        return (x + pltpu.roll(x, side, 1))[:, :side]

    down = []
    for c in range(bounds[-1][0] + bounds[-1][1]):
        even = sum(acc[c] for acc in evens)
        odd = sum(acc[c] for acc in odds)
        down.append(both_sides(jnp.where(left, even, odd)))
    for depth in range(LEVELS - 2, -1, -1):
        lo, size = bounds[depth]
        above = bounds[depth + 1][0]
        for c in range(size):
            parent = jnp.concatenate(split_pair(down[above + c // 2]), axis=1)
            down[lo + c] = down[lo + c] + both_sides(contract(transfer[lo + c], parent, 1, 0))
    for leaf in range(bounds[0][1]):
        block = basis[leaf]
        far_leaf = contract(
            jnp.concatenate(split_pair(down[leaf]), axis=0),
            jnp.concatenate([block, block], axis=0),
            0,
            0,
        )
        out[leaf] = (nbuf[leaf] + far_leaf).astype(BF16)


def far_call(
    bounds, target, listed, coupled, fetched, basis, transfer, near, low, high, blocks,
    chunks=8, flags=None,
):
    peers, pairs, rank, lanes = coupled.shape
    leaves, width, panels = near.shape
    most = chunks * GROUP
    clusters = bounds[-1][0] + bounds[-1][1]
    return pl.pallas_call(
        functools.partial(far_kernel, bounds, chunks),
        grid_spec=pltpu.PrefetchScalarGridSpec(
            num_scalar_prefetch=2,
            grid=(),
            in_specs=[pl.BlockSpec(memory_space=m) for m in (pl.ANY,) * 2 + (pltpu.VMEM,) * 2]
            + [pl.BlockSpec(memory_space=m) for m in (pl.ANY, pltpu.VMEM, pltpu.VMEM, pl.ANY)],
            out_specs=pl.BlockSpec(memory_space=pltpu.VMEM),
            scratch_shapes=[
                pltpu.VMEM(coupled.shape, BF16),
                pltpu.VMEM(fetched.shape, BF16),
                pltpu.VMEM((leaves + 1, width, panels), F32),
                *[pltpu.VMEM((clusters + 1, rank, lanes), F32)] * 4,
                pltpu.VMEM((2 * low.shape[0], width, panels), BF16),
                pltpu.VMEM((most, panels, panels), BF16),
                pltpu.SemaphoreType.DMA((chunks,)),
                pltpu.SemaphoreType.DMA((chunks,)),
                pltpu.SemaphoreType.DMA((3,)),
                pltpu.SemaphoreType.DMA((most,)),
            ],
        ),
        out_shape=jax.ShapeDtypeStruct(near.shape, BF16),
        compiler_params=pltpu.CompilerParams(vmem_limit_bytes=48 << 20, flags=flags or {}),
        name="far",
    )(target, listed, coupled, fetched, basis, transfer, near, low, high, blocks)


def whole(shape):
    return pl.BlockSpec(shape, lambda *_: (0,) * len(shape))


def shards(
    charges, leaf_basis, transfer, near_blocks, near_source, coupling, send_cluster, target_cluster
):
    leaves, panels, width = charges.shape
    rank = leaf_basis.shape[2]
    peers, slots = send_cluster.shape[1:]
    near = near_source.shape[1]
    bounds, clusters = level_bounds(leaves)
    pairs = slots // 2
    lanes = 2 * width
    coupled = coupling[0].reshape(peers, pairs, 2, rank, rank)
    coupled = jnp.swapaxes(coupled, 2, 3).reshape(peers, pairs, rank, 2 * rank)
    reach = leaves // 2
    outer, inner = lax.axis_size("gx"), lax.axis_size("gy")
    count = outer * inner

    charges_t = jnp.swapaxes(charges, 1, 2)
    basis_t = jnp.swapaxes(leaf_basis, 1, 2)
    matrices = transfer[0]
    send = jnp.transpose(send_cluster, (2, 0, 1))
    target = jnp.transpose(target_cluster, (2, 0, 1))
    source = jnp.transpose(near_source, (1, 0))

    up = [(i, i + 1) for i in range(count - 1)]
    low = lax.ppermute(charges_t[leaves - reach :], AXES, up)
    high = lax.ppermute(charges_t[:reach], AXES, [(b, a) for a, b in up])

    chunks = 8
    packed = pl.pallas_call(
        functools.partial(up_kernel, bounds, slots),
        grid_spec=pltpu.PrefetchScalarGridSpec(
            num_scalar_prefetch=1,
            grid=(),
            in_specs=[pl.BlockSpec(memory_space=pltpu.VMEM)] * 3,
            out_specs=pl.BlockSpec(memory_space=pl.ANY),
            scratch_shapes=[
                pltpu.VMEM((clusters, rank, lanes), BF16),
                pltpu.VMEM((chunks, peers * pairs * rank // chunks, lanes), BF16),
                pltpu.SemaphoreType.DMA((chunks,)),
            ],
        ),
        out_shape=jax.ShapeDtypeStruct((peers * pairs * rank, lanes), BF16),
        cost_estimate=pl.CostEstimate(
            flops=2 * leaves * panels * rank * width,
            bytes_accessed=2 * peers * slots * rank * width,
            transcendentals=0,
        ),
        name="up_pick",
    )(send, charges_t, basis_t, matrices)

    fetched = lax.all_to_all(packed, AXES, split_axis=0, concat_axis=0, tiled=True)

    per_step = 4
    first = (lax.axis_index(AXES) * leaves).reshape(1)
    near_field, listed = pl.pallas_call(
        functools.partial(near_kernel, reach),
        grid_spec=pltpu.PrefetchScalarGridSpec(
            num_scalar_prefetch=2,
            grid=(leaves // per_step,),
            in_specs=[
                whole((leaves, width, panels)),
                pl.BlockSpec((per_step, near, panels, panels), lambda i, *_: (i, 0, 0, 0)),
            ],
            out_specs=[
                pl.BlockSpec((per_step, width, panels), lambda i, *_: (i, 0, 0)),
                pl.BlockSpec(memory_space=pltpu.SMEM),
            ],
            scratch_shapes=[pltpu.VMEM((leaves + 2 * reach, width, panels), BF16)],
        ),
        out_shape=[
            jax.ShapeDtypeStruct((leaves, width, panels), F32),
            jax.ShapeDtypeStruct((leaves * near + GROUP + 1,), jnp.int32),
        ],
        cost_estimate=pl.CostEstimate(
            flops=2 * leaves * near * panels * panels * width,
            bytes_accessed=2 * leaves * near * panels * panels,
            transcendentals=0,
        ),
        compiler_params=pltpu.CompilerParams(vmem_limit_bytes=24 << 20),
        name="near",
    )(first, source, charges_t, near_blocks)

    potential_t = far_call(
        bounds, target, listed, coupled, fetched, basis_t, matrices, near_field, low, high, near_blocks
    )
    return jnp.swapaxes(potential_t, 1, 2)


def solution(mesh):
    placed = (
        P(AXES, None, None),
        P(AXES, None, None),
        P(AXES, None, None, None),
        P(AXES, None, None, None),
        P(AXES, None),
        P(AXES, None, None, None, None),
        P(AXES, None, None),
        P(AXES, None, None),
    )
    return jax.shard_map(
        shards, mesh=mesh, in_specs=placed, out_specs=P(AXES, None, None), check_vma=False
    )
```

```python
import functools

import jax
import jax.numpy as jnp
from jax import lax
from jax.experimental import pallas as pl
from jax.experimental.pallas import tpu as pltpu
from jax.sharding import PartitionSpec as P

AXES = ("gx", "gy")
LEVELS = 3
GROUP = 4
F32 = jnp.float32
BF16 = jnp.bfloat16


def level_bounds(leaves):
    bounds, offset = [], 0
    for depth in range(LEVELS):
        bounds.append((offset, leaves >> depth))
        offset += leaves >> depth
    return bounds, offset


def contract(a, b, da, db):
    return lax.dot_general(a, b, (((da,), (db,)), ((), ())), preferred_element_type=F32)


def split_pair(x):
    high = x.astype(BF16)
    return high, (x - high.astype(F32)).astype(BF16)


def left_lanes(shape):
    return lax.broadcasted_iota(jnp.int32, shape, 1) < shape[1] // 2


def up_kernel(bounds, slots, send, charges, basis, transfer, out, upward, staged, sems):
    rank = upward.shape[1]
    chunks, rows = staged.shape[:2]
    pairs = slots // 2
    per_chunk = rows // (pairs * rank)

    def put(c, block):
        block = block.astype(BF16)
        upward[c] = jnp.concatenate([block, block], axis=1)
        return block

    held = []
    for leaf in range(bounds[0][1]):
        held.append(put(leaf, contract(basis[leaf], charges[leaf], 1, 1)))
    for depth in range(LEVELS - 1):
        lo, size = bounds[depth]
        above = bounds[depth + 1][0]
        parents = []
        for c in range(size // 2):
            both = jnp.concatenate([transfer[lo + 2 * c], transfer[lo + 2 * c + 1]], axis=0)
            kids = jnp.concatenate([held[2 * c], held[2 * c + 1]], axis=0)
            parents.append(put(above + c, contract(both, kids, 0, 0)))
        held = parents

    def send_out(j):
        rows_out = out.at[pl.ds(pl.multiple_of(j * rows, rows), rows)]
        return pltpu.make_async_copy(staged.at[j], rows_out, sems.at[j])

    left = left_lanes(upward.shape[1:])

    @pl.loop(0, chunks)
    def _(j):
        def copy(i, carry):
            d = j * per_chunk + i
            for q in range(pairs):
                at = pl.multiple_of((i * pairs + q) * rank, rank)
                even, odd = upward[send[2 * q, 0, d]], upward[send[2 * q + 1, 0, d]]
                staged[j, pl.ds(at, rank), :] = jnp.where(left, even, odd)
            return carry

        lax.fori_loop(0, per_chunk, copy, 0, unroll=16)
        send_out(j).start()

    @pl.loop(0, chunks)
    def _(j):
        send_out(j).wait()


def near_kernel(reach, first, source, own, blocks, out, listed, window):
    step = pl.program_id(0)
    leaves = own.shape[0]
    per_step, near = blocks.shape[:2]

    @pl.when(step == 0)
    def _():
        edge = jnp.zeros((reach, *own.shape[1:]), BF16)
        window[pl.ds(0, reach)] = edge
        window[pl.ds(reach, leaves)] = own[...]
        window[pl.ds(reach + leaves, reach)] = edge

        def note(leaf, found):
            for s in range(near):
                row = source[s, leaf] - first[0]
                inside = (row >= 0) & (row < leaves)
                edge_row = jnp.where(row < 0, row + reach, row - leaves + reach)
                listed[found] = edge_row | (s << 8) | (leaf << 16) | (leaf << 24)
                found = found + jnp.where(inside, 0, 1)
            return found

        most = leaves * near + GROUP

        def clear(i, carry):
            listed[i] = leaves << 24
            return carry

        lax.fori_loop(0, most, clear, 0, unroll=GROUP)
        found = lax.fori_loop(0, leaves, note, 0)
        for i in range(GROUP):
            listed[found + i] = leaves << 24
        listed[most] = (found + GROUP - 1) // GROUP

    for i in range(per_step):
        total = None
        for s in range(near):
            row = source[s, step * per_step + i] - first[0] + reach
            term = contract(window[row], blocks[i, s], 1, 1)
            total = term if total is None else total + term
        out[i] = total


def far_kernel(
    chunks, target, coupling, fetched, out,
    cbuf, fbuf, acc0, acc1, acc2, acc3, csem, fsem,
):
    count, pairs, rank, lanes = coupling.shape
    peers = count // chunks
    rows = peers * pairs * rank

    def fetch(j):
        some = pl.ds(pl.multiple_of(j * peers, peers), peers)
        some_rows = pl.ds(pl.multiple_of(j * rows, rows), rows)
        return (
            pltpu.make_async_copy(fetched.at[some_rows], fbuf.at[some_rows], fsem.at[j]),
            pltpu.make_async_copy(coupling.at[some], cbuf.at[some], csem.at[j]),
        )

    @pl.loop(0, chunks)
    def _(j):
        for copy in fetch(j):
            copy.start()

    evens, odds = (acc0, acc1), (acc2, acc3)
    for acc in evens + odds:
        acc[...] = jnp.zeros_like(acc)
    left = left_lanes((rank, lanes))
    side = lanes // 2

    @pl.loop(0, chunks)
    def _(j):
        for copy in fetch(j):
            copy.wait()
        for i in range(peers):
            p = j * peers + i
            for q in range(pairs):
                v = fbuf[pl.ds(pl.multiple_of((p * pairs + q) * rank, rank), rank), :]
                zero = jnp.zeros_like(v)
                u = jnp.concatenate([jnp.where(left, v, zero), jnp.where(left, zero, v)], axis=0)
                product = contract(cbuf[p, q], u, 1, 0)
                turn = (i * pairs + q) % len(evens)
                evens[turn][target[2 * q, 0, p]] += product
                odds[turn][target[2 * q + 1, 0, p]] += product

    for c in range(out.shape[0]):
        even = sum(acc[c] for acc in evens)
        odd = sum(acc[c] for acc in odds)
        out[c] = jnp.where(left, even, odd)


def edge_kernel(
    bounds, batch, listed, sums, near, basis, transfer, low, high, blocks, out, edge, total, held, sems
):
    leaves, reach = near.shape[0], low.shape[0]
    side = sums.shape[2] // 2
    slots = held.shape[0]
    groups = listed[listed.shape[0] - 1]
    batches = jnp.minimum(slots // batch, (groups * GROUP + batch - 1) // batch)

    def fetch(i, slot):
        entry = listed[i]
        block = blocks.at[(entry >> 16) & 255, (entry >> 8) & 255]
        return pltpu.make_async_copy(block, held.at[slot], sems.at[slot])

    def add(i, slot, count):
        terms = [contract(edge[listed[i + k] & 255], held[slot + k], 1, 1) for k in range(count)]
        for k in range(count):
            total[listed[i + k] >> 24] += terms[k]

    @pl.loop(0, batches * batch)
    def _(i):
        fetch(i, i).start()

    edge[pl.ds(0, reach)] = low[...]
    edge[pl.ds(reach, reach)] = high[...]

    def both_sides(x):
        return (x + pltpu.roll(x, side, 1))[:, :side]

    down = [both_sides(sums[c]) for c in range(sums.shape[0])]
    for depth in range(LEVELS - 2, -1, -1):
        lo, size = bounds[depth]
        above = bounds[depth + 1][0]
        for c in range(size):
            parent = jnp.concatenate(split_pair(down[above + c // 2]), axis=1)
            down[lo + c] = down[lo + c] + both_sides(contract(transfer[lo + c], parent, 1, 0))
    for leaf in range(leaves):
        block = basis[leaf]
        far_leaf = contract(
            jnp.concatenate(split_pair(down[leaf]), axis=0),
            jnp.concatenate([block, block], axis=0),
            0,
            0,
        )
        total[leaf] = near[leaf] + far_leaf

    @pl.loop(0, batches)
    def _(j):
        for k in range(batch):
            fetch(j * batch + k, j * batch + k).wait()
        add(j * batch, j * batch, batch)

    @pl.loop(slots // GROUP, groups)
    def _(g):
        for k in range(GROUP):
            fetch(g * GROUP + k, k).start()
        for k in range(GROUP):
            fetch(g * GROUP + k, k).wait()
        add(g * GROUP, 0, GROUP)

    out[...] = total[pl.ds(0, leaves)].astype(BF16)


def far_call(clusters, target, coupled, fetched, chunks=8):
    peers, pairs, rank, lanes = coupled.shape
    return pl.pallas_call(
        functools.partial(far_kernel, chunks),
        grid_spec=pltpu.PrefetchScalarGridSpec(
            num_scalar_prefetch=1,
            grid=(),
            in_specs=[pl.BlockSpec(memory_space=pl.ANY)] * 2,
            out_specs=pl.BlockSpec(memory_space=pltpu.VMEM),
            scratch_shapes=[
                pltpu.VMEM(coupled.shape, BF16),
                pltpu.VMEM(fetched.shape, BF16),
                *[pltpu.VMEM((clusters + 1, rank, lanes), F32)] * 4,
                pltpu.SemaphoreType.DMA((chunks,)),
                pltpu.SemaphoreType.DMA((chunks,)),
            ],
        ),
        out_shape=jax.ShapeDtypeStruct((clusters, rank, lanes), F32),
        compiler_params=pltpu.CompilerParams(vmem_limit_bytes=48 << 20),
        cost_estimate=pl.CostEstimate(
            flops=4 * fetched.size * rank, bytes_accessed=4 * fetched.size, transcendentals=0
        ),
        name="far",
    )(target, coupled, fetched)


def edge_call(bounds, listed, sums, near, basis, transfer, low, high, blocks, slots=32, batch=8):
    leaves, width, panels = near.shape
    return pl.pallas_call(
        functools.partial(edge_kernel, bounds, batch),
        grid_spec=pltpu.PrefetchScalarGridSpec(
            num_scalar_prefetch=1,
            grid=(),
            in_specs=[pl.BlockSpec(memory_space=pltpu.VMEM)] * 6
            + [pl.BlockSpec(memory_space=pl.ANY)],
            out_specs=pl.BlockSpec(memory_space=pltpu.VMEM),
            scratch_shapes=[
                pltpu.VMEM((2 * low.shape[0], width, panels), BF16),
                pltpu.VMEM((leaves + 1, width, panels), F32),
                pltpu.VMEM((slots, panels, panels), BF16),
                pltpu.SemaphoreType.DMA((slots,)),
            ],
        ),
        out_shape=jax.ShapeDtypeStruct(near.shape, BF16),
        compiler_params=pltpu.CompilerParams(vmem_limit_bytes=48 << 20),
        name="edge",
    )(listed, sums, near, basis, transfer, low, high, blocks)


def whole(shape):
    return pl.BlockSpec(shape, lambda *_: (0,) * len(shape))


def shards(
    charges, leaf_basis, transfer, near_blocks, near_source, coupling, send_cluster, target_cluster
):
    leaves, panels, width = charges.shape
    rank = leaf_basis.shape[2]
    peers, slots = send_cluster.shape[1:]
    near = near_source.shape[1]
    bounds, clusters = level_bounds(leaves)
    pairs = slots // 2
    lanes = 2 * width
    coupled = coupling[0].reshape(peers, pairs, 2, rank, rank)
    coupled = jnp.swapaxes(coupled, 2, 3).reshape(peers, pairs, rank, 2 * rank)
    reach = leaves // 2
    outer, inner = lax.axis_size("gx"), lax.axis_size("gy")
    count = outer * inner

    charges_t = jnp.swapaxes(charges, 1, 2)
    basis_t = jnp.swapaxes(leaf_basis, 1, 2)
    matrices = transfer[0]
    send = jnp.transpose(send_cluster, (2, 0, 1))
    target = jnp.transpose(target_cluster, (2, 0, 1))
    source = jnp.transpose(near_source, (1, 0))

    up = [(i, i + 1) for i in range(count - 1)]
    low = lax.ppermute(charges_t[leaves - reach :], AXES, up)
    high = lax.ppermute(charges_t[:reach], AXES, [(b, a) for a, b in up])

    chunks = 8
    packed = pl.pallas_call(
        functools.partial(up_kernel, bounds, slots),
        grid_spec=pltpu.PrefetchScalarGridSpec(
            num_scalar_prefetch=1,
            grid=(),
            in_specs=[pl.BlockSpec(memory_space=pltpu.VMEM)] * 3,
            out_specs=pl.BlockSpec(memory_space=pl.ANY),
            scratch_shapes=[
                pltpu.VMEM((clusters, rank, lanes), BF16),
                pltpu.VMEM((chunks, peers * pairs * rank // chunks, lanes), BF16),
                pltpu.SemaphoreType.DMA((chunks,)),
            ],
        ),
        out_shape=jax.ShapeDtypeStruct((peers * pairs * rank, lanes), BF16),
        cost_estimate=pl.CostEstimate(
            flops=2 * leaves * panels * rank * width,
            bytes_accessed=2 * peers * slots * rank * width,
            transcendentals=0,
        ),
        name="up_pick",
    )(send, charges_t, basis_t, matrices)

    fetched = lax.all_to_all(packed, AXES, split_axis=0, concat_axis=0, tiled=True)

    per_step = 4
    first = (lax.axis_index(AXES) * leaves).reshape(1)
    near_field, listed = pl.pallas_call(
        functools.partial(near_kernel, reach),
        grid_spec=pltpu.PrefetchScalarGridSpec(
            num_scalar_prefetch=2,
            grid=(leaves // per_step,),
            in_specs=[
                whole((leaves, width, panels)),
                pl.BlockSpec((per_step, near, panels, panels), lambda i, *_: (i, 0, 0, 0)),
            ],
            out_specs=[
                pl.BlockSpec((per_step, width, panels), lambda i, *_: (i, 0, 0)),
                pl.BlockSpec(memory_space=pltpu.SMEM),
            ],
            scratch_shapes=[pltpu.VMEM((leaves + 2 * reach, width, panels), BF16)],
        ),
        out_shape=[
            jax.ShapeDtypeStruct((leaves, width, panels), F32),
            jax.ShapeDtypeStruct((leaves * near + GROUP + 1,), jnp.int32),
        ],
        cost_estimate=pl.CostEstimate(
            flops=2 * leaves * near * panels * panels * width,
            bytes_accessed=2 * leaves * near * panels * panels,
            transcendentals=0,
        ),
        compiler_params=pltpu.CompilerParams(vmem_limit_bytes=24 << 20),
        name="near",
    )(first, source, charges_t, near_blocks)

    sums = far_call(clusters, target, coupled, fetched)
    low, high, sums = lax.optimization_barrier((low, high, sums))
    potential_t = edge_call(
        bounds, listed, sums, near_field, basis_t, matrices, low, high, near_blocks
    )
    return jnp.swapaxes(potential_t, 1, 2)


def solution(mesh):
    placed = (
        P(AXES, None, None),
        P(AXES, None, None),
        P(AXES, None, None, None),
        P(AXES, None, None, None),
        P(AXES, None),
        P(AXES, None, None, None, None),
        P(AXES, None, None),
        P(AXES, None, None),
    )
    return jax.shard_map(
        shards, mesh=mesh, in_specs=placed, out_specs=P(AXES, None, None), check_vma=False
    )
```

```python
import functools

import jax
import jax.numpy as jnp
from jax import lax
from jax.experimental import pallas as pl
from jax.experimental.pallas import tpu as pltpu
from jax.sharding import PartitionSpec as P

AXES = ("gx", "gy")
LEVELS = 3
GROUP = 4
F32 = jnp.float32
BF16 = jnp.bfloat16


def level_bounds(leaves):
    bounds, offset = [], 0
    for depth in range(LEVELS):
        bounds.append((offset, leaves >> depth))
        offset += leaves >> depth
    return bounds, offset


def contract(a, b, da, db):
    return lax.dot_general(a, b, (((da,), (db,)), ((), ())), preferred_element_type=F32)


def split_pair(x):
    high = x.astype(BF16)
    return high, (x - high.astype(F32)).astype(BF16)


def left_lanes(shape):
    return lax.broadcasted_iota(jnp.int32, shape, 1) < shape[1] // 2


def up_kernel(bounds, slots, send, charges, basis, transfer, out, upward, staged, sems):
    rank = upward.shape[1]
    chunks, rows = staged.shape[:2]
    pairs = slots // 2
    per_chunk = rows // (pairs * rank)

    def put(c, block):
        block = block.astype(BF16)
        upward[c] = jnp.concatenate([block, block], axis=1)
        return block

    held = []
    for leaf in range(bounds[0][1]):
        held.append(put(leaf, contract(basis[leaf], charges[leaf], 1, 1)))
    for depth in range(LEVELS - 1):
        lo, size = bounds[depth]
        above = bounds[depth + 1][0]
        parents = []
        for c in range(size // 2):
            both = jnp.concatenate([transfer[lo + 2 * c], transfer[lo + 2 * c + 1]], axis=0)
            kids = jnp.concatenate([held[2 * c], held[2 * c + 1]], axis=0)
            parents.append(put(above + c, contract(both, kids, 0, 0)))
        held = parents

    def send_out(j):
        rows_out = out.at[pl.ds(pl.multiple_of(j * rows, rows), rows)]
        return pltpu.make_async_copy(staged.at[j], rows_out, sems.at[j])

    left = left_lanes(upward.shape[1:])

    @pl.loop(0, chunks)
    def _(j):
        def copy(i, carry):
            d = j * per_chunk + i
            for q in range(pairs):
                at = pl.multiple_of((i * pairs + q) * rank, rank)
                even, odd = upward[send[2 * q, 0, d]], upward[send[2 * q + 1, 0, d]]
                staged[j, pl.ds(at, rank), :] = jnp.where(left, even, odd)
            return carry

        lax.fori_loop(0, per_chunk, copy, 0, unroll=8)
        send_out(j).start()

    @pl.loop(0, chunks)
    def _(j):
        send_out(j).wait()


def near_kernel(reach, first, source, own, blocks, out, listed, window):
    step = pl.program_id(0)
    leaves = own.shape[0]
    per_step, near = blocks.shape[:2]

    @pl.when(step == 0)
    def _():
        edge = jnp.zeros((reach, *own.shape[1:]), BF16)
        window[pl.ds(0, reach)] = edge
        window[pl.ds(reach, leaves)] = own[...]
        window[pl.ds(reach + leaves, reach)] = edge

        def note(leaf, found):
            for s in range(near):
                row = source[s, leaf] - first[0]
                inside = (row >= 0) & (row < leaves)
                edge_row = jnp.where(row < 0, row + reach, row - leaves + reach)
                listed[found] = edge_row | (s << 8) | (leaf << 16) | (leaf << 24)
                found = found + jnp.where(inside, 0, 1)
            return found

        most = leaves * near + GROUP

        def clear(i, carry):
            listed[i] = leaves << 24
            return carry

        lax.fori_loop(0, most, clear, 0, unroll=GROUP)
        found = lax.fori_loop(0, leaves, note, 0)
        for i in range(GROUP):
            listed[found + i] = leaves << 24
        listed[most] = (found + GROUP - 1) // GROUP

    for i in range(per_step):
        total = None
        for s in range(near):
            row = source[s, step * per_step + i] - first[0] + reach
            term = contract(window[row], blocks[i, s], 1, 1)
            total = term if total is None else total + term
        out[i] = total


def far_kernel(
    chunks, target, coupling, fetched, out,
    cbuf, fbuf, acc0, acc1, acc2, acc3, csem, fsem,
):
    count, pairs, rank, lanes = coupling.shape
    peers = count // chunks
    rows = peers * pairs * rank

    def fetch(j):
        some = pl.ds(pl.multiple_of(j * peers, peers), peers)
        some_rows = pl.ds(pl.multiple_of(j * rows, rows), rows)
        return (
            pltpu.make_async_copy(fetched.at[some_rows], fbuf.at[some_rows], fsem.at[j]),
            pltpu.make_async_copy(coupling.at[some], cbuf.at[some], csem.at[j]),
        )

    @pl.loop(0, chunks)
    def _(j):
        for copy in fetch(j):
            copy.start()

    evens, odds = (acc0, acc1), (acc2, acc3)
    for acc in evens + odds:
        acc[...] = jnp.zeros_like(acc)
    left = left_lanes((rank, lanes))
    side = lanes // 2

    @pl.loop(0, chunks)
    def _(j):
        for copy in fetch(j):
            copy.wait()
        for i in range(peers):
            p = j * peers + i
            for q in range(pairs):
                v = fbuf[pl.ds(pl.multiple_of((p * pairs + q) * rank, rank), rank), :]
                zero = jnp.zeros_like(v)
                u = jnp.concatenate([jnp.where(left, v, zero), jnp.where(left, zero, v)], axis=0)
                product = contract(cbuf[p, q], u, 1, 0)
                turn = (i * pairs + q) % len(evens)
                evens[turn][target[2 * q, 0, p]] += product
                odds[turn][target[2 * q + 1, 0, p]] += product

    for c in range(out.shape[0]):
        even = sum(acc[c] for acc in evens)
        odd = sum(acc[c] for acc in odds)
        out[c] = jnp.where(left, even, odd)


def edge_kernel(
    bounds, batch, listed, sums, near, basis, transfer, low, high, blocks, out, edge, total, held, sems
):
    leaves, reach = near.shape[0], low.shape[0]
    side = sums.shape[2] // 2
    slots = held.shape[0]
    groups = listed[listed.shape[0] - 1]
    batches = jnp.minimum(slots // batch, (groups * GROUP + batch - 1) // batch)

    def fetch(i, slot):
        entry = listed[i]
        block = blocks.at[(entry >> 16) & 255, (entry >> 8) & 255]
        return pltpu.make_async_copy(block, held.at[slot], sems.at[slot])

    def add(i, slot, count):
        terms = [contract(edge[listed[i + k] & 255], held[slot + k], 1, 1) for k in range(count)]
        for k in range(count):
            total[listed[i + k] >> 24] += terms[k]

    @pl.loop(0, batches * batch)
    def _(i):
        fetch(i, i).start()

    edge[pl.ds(0, reach)] = low[...]
    edge[pl.ds(reach, reach)] = high[...]

    def both_sides(x):
        return (x + pltpu.roll(x, side, 1))[:, :side]

    down = [both_sides(sums[c]) for c in range(sums.shape[0])]
    for depth in range(LEVELS - 2, -1, -1):
        lo, size = bounds[depth]
        above = bounds[depth + 1][0]
        for c in range(size):
            parent = jnp.concatenate(split_pair(down[above + c // 2]), axis=1)
            down[lo + c] = down[lo + c] + both_sides(contract(transfer[lo + c], parent, 1, 0))
    for leaf in range(leaves):
        block = basis[leaf]
        far_leaf = contract(
            jnp.concatenate(split_pair(down[leaf]), axis=0),
            jnp.concatenate([block, block], axis=0),
            0,
            0,
        )
        total[leaf] = near[leaf] + far_leaf

    @pl.loop(0, batches)
    def _(j):
        for k in range(batch):
            fetch(j * batch + k, j * batch + k).wait()
        add(j * batch, j * batch, batch)

    @pl.loop(slots // GROUP, groups)
    def _(g):
        for k in range(GROUP):
            fetch(g * GROUP + k, k).start()
        for k in range(GROUP):
            fetch(g * GROUP + k, k).wait()
        add(g * GROUP, 0, GROUP)

    out[...] = total[pl.ds(0, leaves)].astype(BF16)


def far_call(clusters, target, coupled, fetched, chunks=4):
    peers, pairs, rank, lanes = coupled.shape
    return pl.pallas_call(
        functools.partial(far_kernel, chunks),
        grid_spec=pltpu.PrefetchScalarGridSpec(
            num_scalar_prefetch=1,
            grid=(),
            in_specs=[pl.BlockSpec(memory_space=pl.ANY)] * 2,
            out_specs=pl.BlockSpec(memory_space=pltpu.VMEM),
            scratch_shapes=[
                pltpu.VMEM(coupled.shape, BF16),
                pltpu.VMEM(fetched.shape, BF16),
                *[pltpu.VMEM((clusters + 1, rank, lanes), F32)] * 4,
                pltpu.SemaphoreType.DMA((chunks,)),
                pltpu.SemaphoreType.DMA((chunks,)),
            ],
        ),
        out_shape=jax.ShapeDtypeStruct((clusters, rank, lanes), F32),
        compiler_params=pltpu.CompilerParams(vmem_limit_bytes=48 << 20),
        cost_estimate=pl.CostEstimate(
            flops=4 * fetched.size * rank, bytes_accessed=4 * fetched.size, transcendentals=0
        ),
        name="far",
    )(target, coupled, fetched)


def edge_call(bounds, listed, sums, near, basis, transfer, low, high, blocks, slots=32, batch=8):
    leaves, width, panels = near.shape
    return pl.pallas_call(
        functools.partial(edge_kernel, bounds, batch),
        grid_spec=pltpu.PrefetchScalarGridSpec(
            num_scalar_prefetch=1,
            grid=(),
            in_specs=[pl.BlockSpec(memory_space=pltpu.VMEM)] * 6
            + [pl.BlockSpec(memory_space=pl.ANY)],
            out_specs=pl.BlockSpec(memory_space=pltpu.VMEM),
            scratch_shapes=[
                pltpu.VMEM((2 * low.shape[0], width, panels), BF16),
                pltpu.VMEM((leaves + 1, width, panels), F32),
                pltpu.VMEM((slots, panels, panels), BF16),
                pltpu.SemaphoreType.DMA((slots,)),
            ],
        ),
        out_shape=jax.ShapeDtypeStruct(near.shape, BF16),
        compiler_params=pltpu.CompilerParams(vmem_limit_bytes=48 << 20),
        name="edge",
    )(listed, sums, near, basis, transfer, low, high, blocks)


def whole(shape):
    return pl.BlockSpec(shape, lambda *_: (0,) * len(shape))


def shards(
    charges, leaf_basis, transfer, near_blocks, near_source, coupling, send_cluster, target_cluster
):
    leaves, panels, width = charges.shape
    rank = leaf_basis.shape[2]
    peers, slots = send_cluster.shape[1:]
    near = near_source.shape[1]
    bounds, clusters = level_bounds(leaves)
    pairs = slots // 2
    lanes = 2 * width
    coupled = coupling[0].reshape(peers, pairs, 2, rank, rank)
    coupled = jnp.swapaxes(coupled, 2, 3).reshape(peers, pairs, rank, 2 * rank)
    reach = leaves // 2
    outer, inner = lax.axis_size("gx"), lax.axis_size("gy")
    count = outer * inner

    charges_t = jnp.swapaxes(charges, 1, 2)
    basis_t = jnp.swapaxes(leaf_basis, 1, 2)
    matrices = transfer[0]
    send = jnp.transpose(send_cluster, (2, 0, 1))
    target = jnp.transpose(target_cluster, (2, 0, 1))
    source = jnp.transpose(near_source, (1, 0))

    up = [(i, i + 1) for i in range(count - 1)]
    low = lax.ppermute(charges_t[leaves - reach :], AXES, up)
    high = lax.ppermute(charges_t[:reach], AXES, [(b, a) for a, b in up])

    chunks = 16
    packed = pl.pallas_call(
        functools.partial(up_kernel, bounds, slots),
        grid_spec=pltpu.PrefetchScalarGridSpec(
            num_scalar_prefetch=1,
            grid=(),
            in_specs=[pl.BlockSpec(memory_space=pltpu.VMEM)] * 3,
            out_specs=pl.BlockSpec(memory_space=pl.ANY),
            scratch_shapes=[
                pltpu.VMEM((clusters, rank, lanes), BF16),
                pltpu.VMEM((chunks, peers * pairs * rank // chunks, lanes), BF16),
                pltpu.SemaphoreType.DMA((chunks,)),
            ],
        ),
        out_shape=jax.ShapeDtypeStruct((peers * pairs * rank, lanes), BF16),
        cost_estimate=pl.CostEstimate(
            flops=2 * leaves * panels * rank * width,
            bytes_accessed=2 * peers * slots * rank * width,
            transcendentals=0,
        ),
        name="up_pick",
    )(send, charges_t, basis_t, matrices)

    fetched = lax.all_to_all(packed, AXES, split_axis=0, concat_axis=0, tiled=True)

    per_step = 8
    first = (lax.axis_index(AXES) * leaves).reshape(1)
    near_field, listed = pl.pallas_call(
        functools.partial(near_kernel, reach),
        grid_spec=pltpu.PrefetchScalarGridSpec(
            num_scalar_prefetch=2,
            grid=(leaves // per_step,),
            in_specs=[
                whole((leaves, width, panels)),
                pl.BlockSpec((per_step, near, panels, panels), lambda i, *_: (i, 0, 0, 0)),
            ],
            out_specs=[
                pl.BlockSpec((per_step, width, panels), lambda i, *_: (i, 0, 0)),
                pl.BlockSpec(memory_space=pltpu.SMEM),
            ],
            scratch_shapes=[pltpu.VMEM((leaves + 2 * reach, width, panels), BF16)],
        ),
        out_shape=[
            jax.ShapeDtypeStruct((leaves, width, panels), F32),
            jax.ShapeDtypeStruct((leaves * near + GROUP + 1,), jnp.int32),
        ],
        cost_estimate=pl.CostEstimate(
            flops=2 * leaves * near * panels * panels * width,
            bytes_accessed=2 * leaves * near * panels * panels,
            transcendentals=0,
        ),
        compiler_params=pltpu.CompilerParams(vmem_limit_bytes=24 << 20),
        name="near",
    )(first, source, charges_t, near_blocks)

    sums = far_call(clusters, target, coupled, fetched)
    low, high, sums = lax.optimization_barrier((low, high, sums))
    potential_t = edge_call(
        bounds, listed, sums, near_field, basis_t, matrices, low, high, near_blocks
    )
    return jnp.swapaxes(potential_t, 1, 2)


def solution(mesh):
    placed = (
        P(AXES, None, None),
        P(AXES, None, None),
        P(AXES, None, None, None),
        P(AXES, None, None, None),
        P(AXES, None),
        P(AXES, None, None, None, None),
        P(AXES, None, None),
        P(AXES, None, None),
    )
    return jax.shard_map(
        shards, mesh=mesh, in_specs=placed, out_specs=P(AXES, None, None), check_vma=False
    )
```
